32 devices in a mesh: groups: 2 (over y), chol: 4 (over z), occ: 4 (over x, core).
Axes of the slice: x: 2, y: 2, z: 4, core: 2. Of those that a mesh axis runs over, the one named last changes fastest.
Arguments:
- chol_rot: bfloat16 [96, 256, 2048], P(('groups', 'chol'), 'occ'), parts along dimension 0, may hold values from -0.1875 to 0.1875
- green: bfloat16 [4, 256, 2048], P('groups', 'occ', 'chol'), parts along dimension 0, may hold values from -6 to 6
Outputs:
- gradient: float32 [256, 4, 2048], P('occ', 'groups', 'chol'), parts along dimension 1
The draws below stay inside these ranges and needn't reach their ends.
There are 2 independent parts, one for each index of `groups`. The reference program is written for one: setup_inputs(seed, part) draws one part's arguments, and reference() takes and returns one part's arrays. A program takes and returns all parts, laid end to end along the dimension named above; each array names one. Nothing has to cross between parts.
All inputs are finite; a program needn't handle non-finite values.
Results may differ from the reference program's by a relative error of at most 0.0085.
Values may be sent and summed in bfloat16 or wider, within the bound.
No kernel may reach another device: no remote copies, remote signals or barrier semaphores. Data moves between devices by JAX's collectives and lax.ppermute only.
A program may use at most 64 MiB of HBM per device.

```python
import math
import jax
import jax.numpy as jnp
from jax import lax

O = 256
M = 2048
WALKERS = 2
NCHOL = 48
N_CHOL = 4
N_OCC = 4


def raised(entries, stream_key, source, target, blocks, factor):
    def block_of(position):
        return (jnp.arange(entries.shape[position]) // (entries.shape[position] // blocks)).reshape((-1,) + (1,) * (entries.ndim - 1 - position))

    near = jax.random.permutation(stream_key, blocks)[block_of(target)]
    second = (block_of(target) + blocks // 2) % blocks
    return jnp.where((block_of(source) == near) | (block_of(source) == second), factor * entries, entries)


def level_of(key, dims, cuts, smallest, top_value):
    def one(position, shards_of):
        draws = jax.random.uniform(jax.random.fold_in(jax.random.fold_in(key, 6), position), (shards_of,), jnp.float32, smallest / len(cuts), top_value / len(cuts))
        return jnp.repeat(jnp.exp(draws), dims[position] // shards_of).reshape((-1,) + (1,) * (len(dims) - position - 1))

    loudness = one(*cuts[0])
    for cut in cuts[1:]:
        loudness = loudness * one(*cut)
    return loudness


def gaussian(own_key, dims, scale, reach, split=(), held_as=jnp.bfloat16):
    factor_of = level_of(own_key, dims, split, -0.22, 0.18) if split else 1.0
    result = jax.random.normal(own_key, dims, jnp.float32) * scale * factor_of
    return jnp.minimum(jnp.maximum(result, -reach), reach).astype(held_as)


def heavy_noise(stream_key, shape, width, most, pieces, heavy, kind=jnp.bfloat16):
    array = width * jax.random.normal(stream_key, shape, jnp.float32)
    if pieces:
        array = array * level_of(stream_key, shape, pieces, -0.22, 0.18)
    return jnp.clip(raised(array, jax.random.fold_in(stream_key, 3), *heavy), -most, most).astype(kind)


def setup_inputs(seed: int = 0, part: int = 0) -> dict:
    key_of = jax.random.split(jax.random.key(seed), 3)
    part_splits = jax.random.split(jax.random.fold_in(key_of[2], part), 3)
    return {
        "chol_rot": heavy_noise(part_splits[0], (NCHOL, O, M), M ** -0.5, 0.1875, ((0, 4), (1, 4)), (0, 2, 4, 2.0)),
        "green": gaussian(part_splits[1], (WALKERS, O, M), 1.0, 6.0, ((1, 4), (2, 4))),
    }


def reference(chol_rot, green):
    nvec, occupied, orbitals = chol_rot.shape
    walkers = green.shape[0]
    pairs = jnp.dot(chol_rot.reshape(nvec * occupied, orbitals), green.reshape(walkers * occupied, orbitals).T, preferred_element_type=jnp.float32).astype(jnp.bfloat16).reshape(nvec, occupied, walkers, occupied)
    chol_loc = nvec // N_CHOL
    occ_loc = occupied // N_OCC

    def per_block(running, index):
        start = (index * chol_loc).astype(jnp.int32)
        pair_blk = lax.dynamic_slice_in_dim(pairs, start, chol_loc, 0)
        vec_blk = lax.dynamic_slice_in_dim(chol_rot, start, chol_loc, 0)
        for quarter in range(N_OCC):
            pair_q = pair_blk[:, :, :, quarter * occ_loc:(quarter + 1) * occ_loc].astype(jnp.float32)
            vec_q = vec_blk[:, quarter * occ_loc:(quarter + 1) * occ_loc, :].astype(jnp.float32)
            partial_value = jnp.einsum('gjwi,gip->jwp', pair_q, vec_q).astype(jnp.bfloat16)
            partial_value = lax.optimization_barrier(partial_value)
            running = running + partial_value.astype(jnp.float32)
        return (running, None)
    summed, _ = lax.scan(per_block, jnp.zeros((occupied, walkers, orbitals), jnp.float32), jnp.arange(N_CHOL, dtype=jnp.int32))
    return summed * -math.sqrt(orbitals / (nvec * occupied))
```

```python
import functools
import math

import jax
import jax.numpy as jnp
from jax import lax
from jax.experimental import pallas as pl
from jax.experimental.pallas import tpu as pltpu
from jax.sharding import PartitionSpec as P

BF16 = jnp.bfloat16
F32 = jnp.float32


def general(chol_rot, green):
    chol_loc, occ_loc, orbitals = chol_rot.shape
    walkers = green.shape[0]
    occupied = occ_loc * lax.axis_size("occ")
    nvec = chol_loc * lax.axis_size("chol")
    factor = -math.sqrt(orbitals / (nvec * occupied))
    vec_mat = chol_rot.reshape(chol_loc * occ_loc, orbitals)
    green_all = lax.all_gather(green, "occ", axis=1, tiled=True)
    piece = lax.all_gather(green_all, "chol", axis=2, tiled=True)
    flat = piece.reshape(-1, piece.shape[2])
    pair_sum = jnp.dot(vec_mat, flat.T, preferred_element_type=F32)
    pairs = pair_sum.astype(BF16).reshape(chol_loc, occ_loc, walkers, occupied)
    swapped = lax.all_to_all(pairs, "occ", split_axis=3, concat_axis=1, tiled=True)
    partial = jnp.einsum("gjwi,gip->jwp", swapped, chol_rot, preferred_element_type=F32)
    occ_summed = lax.psum_scatter(
        partial.astype(BF16), "occ", scatter_dimension=0, tiled=True
    ).astype(F32)
    summed = lax.psum_scatter(occ_summed, "chol", scatter_dimension=2, tiled=True)
    return summed * factor


def xor_permute(x, axis, bits):
    size = lax.axis_size(axis)
    return lax.ppermute(x, axis, [(i, i ^ bits) for i in range(size)])


def pair_kernel(walkers, occ_loc, vecs, blocks, where_ref, own_ref, sib_ref, *refs):
    green_refs, (near_ref, far_ref), flat = refs[: 2 * blocks], refs[2 * blocks : 2 * blocks + 2], refs[-1]
    width = flat.shape[1] // blocks
    rows = walkers * occ_loc

    @pl.when((pl.program_id(0) == 0) & (pl.program_id(1) == 0))
    def _():
        for side in range(2):
            for r in range(blocks):
                start = pl.multiple_of(where_ref[r] * width, width)
                flat[pl.ds(side * rows, rows), pl.ds(start, width)] = green_refs[side * blocks + r][...]

    def body(vec_ref):
        sums = lax.dot_general(
            vec_ref[...], flat[...], (((1,), (1,)), ((), ())), preferred_element_type=F32
        ).astype(BF16)
        for side, out_ref in enumerate((near_ref, far_ref)):
            for w in range(walkers):
                lane = side * rows + w * occ_loc
                tiles = [sums[g * occ_loc : (g + 1) * occ_loc, lane : lane + occ_loc] for g in range(vecs)]
                out_ref[0, w] = jnp.concatenate(tiles, axis=1)

    @pl.when(pl.program_id(0) == 0)
    def _():
        body(own_ref)

    @pl.when(pl.program_id(0) == 1)
    def _():
        body(sib_ref)


def pair_products(where, own, sib, greens, walkers, occ_loc, vecs):
    total, orbitals = own.shape
    chol_loc = total // occ_loc
    steps = chol_loc // vecs
    blocks = len(greens) // 2
    shape = jax.ShapeDtypeStruct((2, walkers, occ_loc, total), BF16)
    green_spec = pl.BlockSpec(greens[0].shape, lambda t, i, w: (0, 0))
    out_spec = pl.BlockSpec((1, walkers, occ_loc, vecs * occ_loc), lambda t, i, w: (t, 0, 0, i))
    return pl.pallas_call(
        functools.partial(pair_kernel, walkers, occ_loc, vecs, blocks),
        out_shape=(shape, shape),
        grid_spec=pltpu.PrefetchScalarGridSpec(
            num_scalar_prefetch=1,
            grid=(2, steps),
            in_specs=[
                pl.BlockSpec((vecs * occ_loc, orbitals), lambda t, i, w: (jnp.where(t == 0, i, steps - 1), 0)),
                pl.BlockSpec((vecs * occ_loc, orbitals), lambda t, i, w: (jnp.where(t == 0, 0, i), 0)),
            ]
            + [green_spec] * len(greens),
            out_specs=(out_spec, out_spec),
            scratch_shapes=[pltpu.VMEM((2 * walkers * occ_loc, orbitals), BF16)],
        ),
        cost_estimate=pl.CostEstimate(
            flops=2 * 2 * total * orbitals * 2 * walkers * occ_loc,
            bytes_accessed=4 * total * orbitals + 4 * walkers * occ_loc * orbitals + 4 * shape.size,
            transcendentals=0,
        ),
        compiler_params=pltpu.CompilerParams(vmem_limit_bytes=14 << 20),
        name="pairs",
    )(where, own, sib, *greens)


def partial_kernel(where_ref, near_ref, far_ref, vec_ref, keep_near_ref, keep_far_ref, send_ref):
    del where_ref
    rows = keep_near_ref.shape[0]
    for side, (left_ref, keep_ref) in enumerate(((near_ref, keep_near_ref), (far_ref, keep_far_ref))):
        sums = jnp.dot(left_ref[...], vec_ref[...], preferred_element_type=F32).astype(BF16)
        keep_ref[...] = sums[:rows]
        send_ref[pl.ds(side * rows, rows), :] = sums[rows:]


def partial_products(where, r, near, far, own, width):
    rows, total = near.shape
    half = rows // 2
    keep = jax.ShapeDtypeStruct((half, width), BF16)
    send = jax.ShapeDtypeStruct((rows, width), BF16)
    whole = lambda shape: pl.BlockSpec(shape, lambda i, w: (0, 0))
    return pl.pallas_call(
        partial_kernel,
        out_shape=(keep, keep, send),
        grid_spec=pltpu.PrefetchScalarGridSpec(
            num_scalar_prefetch=1,
            grid=(1,),
            in_specs=[whole(near.shape), whole(far.shape), pl.BlockSpec((total, width), lambda i, w: (0, w[r]))],
            out_specs=(whole(keep.shape), whole(keep.shape), whole(send.shape)),
        ),
        cost_estimate=pl.CostEstimate(
            flops=2 * 2 * rows * total * width,
            bytes_accessed=4 * rows * total + 2 * total * width + 4 * rows * width,
            transcendentals=0,
        ),
        compiler_params=pltpu.CompilerParams(vmem_limit_bytes=8 << 20),
        name="partial",
    )(where, near, far, own)


def finish_kernel(factor, first_ref, second_ref, third_ref, *refs):
    out_ref = refs[-1]
    occ_loc, walkers, _ = out_ref.shape
    total = first_ref[...].astype(F32) + second_ref[...].astype(F32) + third_ref[...].astype(F32)
    for ref in refs[:-1]:
        total = total + ref[...].astype(F32)
    total = total * factor
    for w in range(walkers):
        out_ref[:, w, :] = total[w * occ_loc : (w + 1) * occ_loc]


def relative(chol_rot, green):
    chol_loc, occ_loc, orbitals = chol_rot.shape
    walkers, _, width = green.shape
    n_chol = lax.axis_size("chol")
    occupied = occ_loc * lax.axis_size("occ")
    factor = -math.sqrt(orbitals / (chol_loc * n_chol * occupied))
    total = chol_loc * occ_loc
    rows = walkers * occ_loc
    vecs = max(v for v in (4, 2, 1) if chol_loc % v == 0)

    where = lax.axis_index("chol") ^ jnp.arange(n_chol, dtype=jnp.int32)
    own = chol_rot.reshape(total, orbitals)
    sib = xor_permute(own, "occ", 1)
    block = green.reshape(rows, width)
    near = [block] + [xor_permute(block, "chol", r) for r in range(1, n_chol)]
    far = [xor_permute(piece, "occ", 2) for piece in near]
    stay, leave = pair_products(where, own, sib, near + far, walkers, occ_loc, vecs)
    come = xor_permute(leave.reshape(2 * rows, total), "occ", 2)
    stay = stay.reshape(2 * rows, total)

    arrived = []
    for r in reversed(range(n_chol)):
        keep_near, keep_far, send = partial_products(where, r, stay, come, own, width)
        got = xor_permute(send, "occ", 1)
        over = (keep_far.astype(F32) + got[rows:].astype(F32)).astype(BF16)
        crossed = xor_permute(over, "occ", 2)
        if r:
            here = keep_near.astype(F32) + got[:rows].astype(F32) + crossed.astype(F32)
            arrived.append(xor_permute(here.astype(BF16), "chol", r))
        else:
            mine = (keep_near, got[:rows], crossed)

    return pl.pallas_call(
        functools.partial(finish_kernel, factor),
        out_shape=jax.ShapeDtypeStruct((occ_loc, walkers, width), F32),
        compiler_params=pltpu.CompilerParams(vmem_limit_bytes=4 << 20),
        name="finish",
    )(*mine, *arrived)


def local(chol_rot, green):
    occ_loc, width = chol_rot.shape[1], green.shape[2]
    n_chol = lax.axis_size("chol")
    fits = (
        lax.axis_size("occ") == 4
        and n_chol & (n_chol - 1) == 0
        and width % 128 == 0
        and occ_loc % 16 == 0
        and (chol_rot.shape[0] * occ_loc) % 128 == 0
    )
    return relative(chol_rot, green) if fits else general(chol_rot, green)


def solution(mesh):
    return jax.shard_map(
        local,
        mesh=mesh,
        in_specs=(P(("groups", "chol"), "occ", None), P("groups", "occ", "chol")),
        out_specs=P("occ", "groups", "chol"),
        check_vma=False,
    )
```

```python
import functools
import math

import jax
import jax.numpy as jnp
from jax import lax
from jax.experimental import pallas as pl
from jax.experimental.pallas import tpu as pltpu
from jax.sharding import PartitionSpec as P


BF16 = jnp.bfloat16
F32 = jnp.float32


def general(chol_rot, green):
    chol_loc, occ_loc, orbitals = chol_rot.shape
    walkers = green.shape[0]
    occupied = occ_loc * lax.axis_size("occ")
    nvec = chol_loc * lax.axis_size("chol")
    factor = -math.sqrt(orbitals / (nvec * occupied))
    vec_mat = chol_rot.reshape(chol_loc * occ_loc, orbitals)
    green_all = lax.all_gather(green, "occ", axis=1, tiled=True)
    piece = lax.all_gather(green_all, "chol", axis=2, tiled=True)
    flat = piece.reshape(-1, piece.shape[2])
    pair_sum = jnp.dot(vec_mat, flat.T, preferred_element_type=F32)
    pairs = pair_sum.astype(BF16).reshape(chol_loc, occ_loc, walkers, occupied)
    swapped = lax.all_to_all(pairs, "occ", split_axis=3, concat_axis=1, tiled=True)
    partial = jnp.einsum("gjwi,gip->jwp", swapped, chol_rot, preferred_element_type=F32)
    occ_summed = lax.psum_scatter(
        partial.astype(BF16), "occ", scatter_dimension=0, tiled=True
    ).astype(F32)
    summed = lax.psum_scatter(occ_summed, "chol", scatter_dimension=2, tiled=True)
    return summed * factor


def xor_permute(x, axis, bits):
    size = lax.axis_size(axis)
    return lax.ppermute(x, axis, [(i, i ^ bits) for i in range(size)])


def after(x, earlier):
    return lax.optimization_barrier((x, earlier))[0]


VMEM = pl.BlockSpec(memory_space=pltpu.VMEM)
SMEM = pl.BlockSpec(memory_space=pltpu.SMEM)


def stage_kernel(from_ref, to_ref, sem):
    copy = pltpu.make_async_copy(from_ref, to_ref, sem)
    copy.start()
    copy.wait()


def stage(x):
    return pl.pallas_call(
        stage_kernel,
        out_shape=jax.ShapeDtypeStruct(x.shape, x.dtype),
        in_specs=[pl.BlockSpec(memory_space=pltpu.HBM)],
        out_specs=VMEM,
        scratch_shapes=[pltpu.SemaphoreType.DMA],
        compiler_params=pltpu.CompilerParams(vmem_limit_bytes=4 << 20),
        cost_estimate=pl.CostEstimate(flops=0, bytes_accessed=4 * x.size, transcendentals=0),
        name="stage",
    )(x)


def pair_kernel(walkers, occ_loc, blocks, where_ref, own_ref, sib_ref, *refs):
    green_refs, (near_ref, far_ref), flat = refs[: 2 * blocks], refs[2 * blocks : 2 * blocks + 2], refs[-1]
    width = flat.shape[1] // blocks
    rows = walkers * occ_loc
    for side in range(2):
        for r in range(blocks):
            start = pl.multiple_of((where_ref[0] ^ r) * width, width)
            flat[pl.ds(side * rows, rows), pl.ds(start, width)] = green_refs[side * blocks + r][...]
    for core, vec_ref in enumerate((own_ref, sib_ref)):
        sums = lax.dot_general(
            vec_ref[...], flat[...], (((1,), (1,)), ((), ())), preferred_element_type=F32
        ).astype(BF16)
        for side, out_ref in enumerate((near_ref, far_ref)):
            for w in range(walkers):
                lane = side * rows + w * occ_loc
                tiles = [
                    sums[start : start + occ_loc, lane : lane + occ_loc]
                    for start in range(0, sums.shape[0], occ_loc)
                ]
                first = core * rows + w * occ_loc
                out_ref[first : first + occ_loc, :] = jnp.concatenate(tiles, axis=1)


def pair_products(where, own, sib, greens, walkers, occ_loc):
    total, orbitals = own.shape
    rows = walkers * occ_loc
    shape = jax.ShapeDtypeStruct((2 * rows, total), BF16)
    return pl.pallas_call(
        functools.partial(pair_kernel, walkers, occ_loc, len(greens) // 2),
        out_shape=(shape, shape),
        in_specs=[SMEM] + [VMEM] * (2 + len(greens)),
        out_specs=(VMEM, VMEM),
        scratch_shapes=[pltpu.VMEM((2 * rows, orbitals), BF16)],
        compiler_params=pltpu.CompilerParams(vmem_limit_bytes=14 << 20),
        cost_estimate=pl.CostEstimate(
            flops=8 * total * orbitals * rows,
            bytes_accessed=4 * total * orbitals + 4 * rows * orbitals + 4 * shape.size,
            transcendentals=0,
        ),
        name="pairs",
    )(where, own, sib, *greens)


def partial_kernel(which, where_ref, left_ref, vec_ref, *refs):
    keep_refs, send_ref = refs[:-1], refs[-1]
    rows, width = keep_refs[0].shape
    for n, r in enumerate(which):
        start = pl.multiple_of((where_ref[0] ^ r) * width, width)
        sums = jnp.dot(left_ref[...], vec_ref[:, pl.ds(start, width)], preferred_element_type=F32).astype(BF16)
        keep_refs[n][...] = sums[:rows]
        send_ref[n * rows : (n + 1) * rows, :] = sums[rows:]


def partial_products(which, where, left, own, width):
    rows, total = left.shape
    half = rows // 2
    keep = jax.ShapeDtypeStruct((half, width), BF16)
    send = jax.ShapeDtypeStruct((half * len(which), width), BF16)
    call = pl.pallas_call(
        functools.partial(partial_kernel, which),
        out_shape=(keep,) * len(which) + (send,),
        in_specs=[SMEM, VMEM, VMEM],
        out_specs=(VMEM,) * (len(which) + 1),
        compiler_params=pltpu.CompilerParams(vmem_limit_bytes=10 << 20),
        cost_estimate=pl.CostEstimate(
            flops=2 * rows * total * width * len(which),
            bytes_accessed=2 * rows * total + 2 * total * width * len(which) + 2 * rows * width * len(which),
            transcendentals=0,
        ),
        name="partial",
    )
    *keeps, send = call(where, left, own)
    got = xor_permute(send, "occ", 1)
    return {r: (keeps[n], got[n * half : (n + 1) * half]) for n, r in enumerate(which)}


def finish_kernel(factor, *refs):
    out_ref = refs[-1]
    occ_loc, walkers, _ = out_ref.shape
    total = refs[0][...].astype(F32)
    for ref in refs[1:-1]:
        total = total + ref[...].astype(F32)
    total = total * factor
    for w in range(walkers):
        out_ref[:, w, :] = total[w * occ_loc : (w + 1) * occ_loc]


def relative(chol_rot, green):
    chol_loc, occ_loc, orbitals = chol_rot.shape
    walkers, _, width = green.shape
    n_chol = lax.axis_size("chol")
    occupied = occ_loc * lax.axis_size("occ")
    factor = -math.sqrt(orbitals / (chol_loc * n_chol * occupied))
    total = chol_loc * occ_loc
    rows = walkers * occ_loc

    where = lax.axis_index("chol").astype(jnp.int32).reshape(1)
    chol_rot, green = after(chol_rot, where), after(green, where)
    sib = xor_permute(chol_rot.reshape(total, orbitals), "occ", 1)
    own = stage(chol_rot.reshape(total, orbitals))
    near = {0: green.reshape(rows, width)}
    bit = n_chol // 2
    while bit:
        near |= {r | bit: xor_permute(piece, "chol", bit) for r, piece in near.items()}
        if bit * 2 == n_chol:
            near[bit] = after(near[bit], own)
        bit //= 2
    far = {r: xor_permute(near[r], "occ", 2) for r in range(n_chol)}
    greens = [side[r] for side in (near, far) for r in range(n_chol)]
    stay, leave = pair_products(where, own, sib, greens, walkers, occ_loc)
    come = xor_permute(leave, "occ", 2)

    order = tuple(reversed(range(n_chol)))
    half = (n_chol + 1) // 2
    here = partial_products(order, where, stay, own, width)
    come = after(come, here[0][0])
    there = partial_products(order[:half], where, come, own, width)
    there |= partial_products(order[half:], where, come, own, width)
    add = lambda pair: pair[0].astype(F32) + pair[1].astype(F32)
    arrived = []
    for r in order:
        crossed = xor_permute(add(there[r]).astype(BF16), "occ", 2)
        if r:
            if arrived:
                crossed = after(crossed, ready)
            ready = (add(here[r]) + crossed.astype(F32)).astype(BF16)
            arrived.append(xor_permute(ready, "chol", r))
        else:
            mine = (*here[r], crossed)

    return pl.pallas_call(
        functools.partial(finish_kernel, factor),
        out_shape=jax.ShapeDtypeStruct((occ_loc, walkers, width), F32),
        compiler_params=pltpu.CompilerParams(vmem_limit_bytes=4 << 20),
        name="finish",
    )(*mine, *arrived)


def local(chol_rot, green):
    occ_loc, width = chol_rot.shape[1], green.shape[2]
    n_chol = lax.axis_size("chol")
    fits = (
        lax.axis_size("occ") == 4
        and n_chol & (n_chol - 1) == 0
        and width % 128 == 0
        and occ_loc % 16 == 0
        and (chol_rot.shape[0] * occ_loc) % 128 == 0
    )
    return relative(chol_rot, green) if fits else general(chol_rot, green)


def solution(mesh):
    return jax.shard_map(
        local,
        mesh=mesh,
        in_specs=(P(("groups", "chol"), "occ", None), P("groups", "occ", "chol")),
        out_specs=P("occ", "groups", "chol"),
        check_vma=False,
    )
```

```python
import functools
import math

import jax
import jax.numpy as jnp
from jax import lax
from jax.experimental import pallas as pl
from jax.experimental.pallas import tpu as pltpu
from jax.sharding import PartitionSpec as P


BF16 = jnp.bfloat16
F32 = jnp.float32


def general(chol_rot, green):
    chol_loc, occ_loc, orbitals = chol_rot.shape
    walkers = green.shape[0]
    occupied = occ_loc * lax.axis_size("occ")
    nvec = chol_loc * lax.axis_size("chol")
    factor = -math.sqrt(orbitals / (nvec * occupied))
    vec_mat = chol_rot.reshape(chol_loc * occ_loc, orbitals)
    green_all = lax.all_gather(green, "occ", axis=1, tiled=True)
    piece = lax.all_gather(green_all, "chol", axis=2, tiled=True)
    flat = piece.reshape(-1, piece.shape[2])
    pair_sum = jnp.dot(vec_mat, flat.T, preferred_element_type=F32)
    pairs = pair_sum.astype(BF16).reshape(chol_loc, occ_loc, walkers, occupied)
    swapped = lax.all_to_all(pairs, "occ", split_axis=3, concat_axis=1, tiled=True)
    partial = jnp.einsum("gjwi,gip->jwp", swapped, chol_rot, preferred_element_type=F32)
    occ_summed = lax.psum_scatter(
        partial.astype(BF16), "occ", scatter_dimension=0, tiled=True
    ).astype(F32)
    summed = lax.psum_scatter(occ_summed, "chol", scatter_dimension=2, tiled=True)
    return summed * factor


def xor_permute(x, axis, bits):
    size = lax.axis_size(axis)
    return lax.ppermute(x, axis, [(i, i ^ bits) for i in range(size)])


def after(x, earlier):
    return lax.optimization_barrier((x, earlier))[0]


VMEM = pl.BlockSpec(memory_space=pltpu.VMEM)
SMEM = pl.BlockSpec(memory_space=pltpu.SMEM)


def stage_kernel(from_ref, to_ref, sem):
    copy = pltpu.make_async_copy(from_ref, to_ref, sem)
    copy.start()
    copy.wait()


def stage(x):
    return pl.pallas_call(
        stage_kernel,
        out_shape=jax.ShapeDtypeStruct(x.shape, x.dtype),
        in_specs=[pl.BlockSpec(memory_space=pltpu.HBM)],
        out_specs=VMEM,
        scratch_shapes=[pltpu.SemaphoreType.DMA],
        compiler_params=pltpu.CompilerParams(vmem_limit_bytes=4 << 20),
        cost_estimate=pl.CostEstimate(flops=0, bytes_accessed=4 * x.size, transcendentals=0),
        name="stage",
    )(x)


def pair_kernel(walkers, occ_loc, blocks, where_ref, own_ref, sib_ref, *refs):
    green_refs, (near_ref, far_ref), flat = refs[: 2 * blocks], refs[2 * blocks : 2 * blocks + 2], refs[-1]
    width = flat.shape[1] // blocks
    rows = walkers * occ_loc
    for side in range(2):
        for r in range(blocks):
            start = pl.multiple_of((where_ref[0] ^ r) * width, width)
            flat[pl.ds(side * rows, rows), pl.ds(start, width)] = green_refs[side * blocks + r][...]
    for core, vec_ref in enumerate((own_ref, sib_ref)):
        sums = lax.dot_general(
            vec_ref[...], flat[...], (((1,), (1,)), ((), ())), preferred_element_type=F32
        ).astype(BF16)
        for side, out_ref in enumerate((near_ref, far_ref)):
            for w in range(walkers):
                lane = side * rows + w * occ_loc
                tiles = [
                    sums[start : start + occ_loc, lane : lane + occ_loc]
                    for start in range(0, sums.shape[0], occ_loc)
                ]
                first = core * rows + w * occ_loc
                out_ref[first : first + occ_loc, :] = jnp.concatenate(tiles, axis=1)


def pair_products(where, own, sib, greens, walkers, occ_loc):
    total, orbitals = own.shape
    rows = walkers * occ_loc
    shape = jax.ShapeDtypeStruct((2 * rows, total), BF16)
    return pl.pallas_call(
        functools.partial(pair_kernel, walkers, occ_loc, len(greens) // 2),
        out_shape=(shape, shape),
        in_specs=[SMEM] + [VMEM] * (2 + len(greens)),
        out_specs=(VMEM, VMEM),
        scratch_shapes=[pltpu.VMEM((2 * rows, orbitals), BF16)],
        compiler_params=pltpu.CompilerParams(vmem_limit_bytes=14 << 20),
        cost_estimate=pl.CostEstimate(
            flops=8 * total * orbitals * rows,
            bytes_accessed=4 * total * orbitals + 4 * rows * orbitals + 4 * shape.size,
            transcendentals=0,
        ),
        name="pairs",
    )(where, own, sib, *greens)


def partial_kernel(which, where_ref, left_ref, vec_ref, keep_ref, send_ref):
    width = keep_ref.shape[1]
    rows = left_ref.shape[0] // 2
    for n, r in enumerate(which):
        start = pl.multiple_of((where_ref[0] ^ r) * width, width)
        sums = jnp.dot(left_ref[...], vec_ref[:, pl.ds(start, width)], preferred_element_type=F32).astype(BF16)
        keep_ref[n * rows : (n + 1) * rows, :] = sums[:rows]
        send_ref[n * rows : (n + 1) * rows, :] = sums[rows:]


def partial_products(which, where, left, own, width):
    rows, total = left.shape
    out = jax.ShapeDtypeStruct((rows // 2 * len(which), width), BF16)
    call = pl.pallas_call(
        functools.partial(partial_kernel, which),
        out_shape=(out, out),
        in_specs=[SMEM, VMEM, VMEM],
        out_specs=(VMEM, VMEM),
        compiler_params=pltpu.CompilerParams(vmem_limit_bytes=10 << 20),
        cost_estimate=pl.CostEstimate(
            flops=4 * out.size * total,
            bytes_accessed=2 * rows * total + 2 * total * width * len(which) + 4 * out.size,
            transcendentals=0,
        ),
        name="partial",
    )
    keep, send = call(where, left, own)
    return keep, xor_permute(send, "occ", 1)


def finish_kernel(factor, keep_ref, got_ref, *refs):
    out_ref = refs[-1]
    occ_loc, walkers, _ = out_ref.shape
    rows = walkers * occ_loc
    total = keep_ref[-rows:].astype(F32) + got_ref[-rows:].astype(F32)
    for ref in refs[:-1]:
        total = total + ref[-rows:].astype(F32)
    total = total * factor
    for w in range(walkers):
        out_ref[:, w, :] = total[w * occ_loc : (w + 1) * occ_loc]


def relative(chol_rot, green):
    chol_loc, occ_loc, orbitals = chol_rot.shape
    walkers, _, width = green.shape
    n_chol = lax.axis_size("chol")
    occupied = occ_loc * lax.axis_size("occ")
    factor = -math.sqrt(orbitals / (chol_loc * n_chol * occupied))
    total = chol_loc * occ_loc
    rows = walkers * occ_loc

    where = lax.axis_index("chol").astype(jnp.int32).reshape(1)
    chol_rot, green = after(chol_rot, where), after(green, where)
    sib = xor_permute(chol_rot.reshape(total, orbitals), "occ", 1)
    own = stage(chol_rot.reshape(total, orbitals))
    near = {0: green.reshape(rows, width)}
    far = {0: xor_permute(near[0], "occ", 2)}
    bit = n_chol // 2
    while bit:
        near |= {r | bit: xor_permute(piece, "chol", bit) for r, piece in near.items()}
        if bit * 2 == n_chol:
            near[bit] = after(near[bit], own)
        bit //= 2
    for r in range(1, n_chol):
        if r == 1:
            far[r] = xor_permute(far[0], "chol", r)
        else:
            far[r] = xor_permute(near[r], "occ", 2)
    greens = [side[r] for side in (near, far) for r in range(n_chol)]
    stay, leave = pair_products(where, own, sib, greens, walkers, occ_loc)
    come = xor_permute(leave, "occ", 2)

    odds = tuple(range(n_chol - 1, 0, -2))
    evens = tuple(r - 1 for r in odds)

    def part(x, n):
        return x[n * rows : (n + 1) * rows].astype(F32)

    near_keep, near_got = partial_products(odds + evens, where, stay, own, width)
    half = len(odds) * rows
    near_odd = (near_keep[:half].astype(F32) + near_got[:half].astype(F32)).astype(BF16)
    come = after(come, near_odd)
    near_came = xor_permute(near_odd, "chol", 1)
    far = {}
    for which in (odds[:1], odds[1:] + evens):
        pair = partial_products(which, where, come, own, width)
        far |= {r: part(pair[0], n) + part(pair[1], n) for n, r in enumerate(which)}
    far |= {r - 1: far[r - 1] + xor_permute(far[r].astype(BF16), "chol", 1).astype(F32) for r in odds}
    crossed = {r: xor_permute(far[r].astype(BF16), "occ", 2) for r in evens}
    summed = {
        r: part(near_keep, len(odds) + n) + part(near_got, len(odds) + n) + part(near_came, n)
        + crossed[r].astype(F32)
        for n, r in enumerate(evens) if r
    }
    came = []
    bit = n_chol // 2
    while bit > 1:
        for r in evens:
            if r & bit and r < 2 * bit:
                moved = xor_permute(summed[r].astype(BF16), "chol", bit)
                if r == bit:
                    came.append(moved)
                else:
                    summed[r ^ bit] = summed[r ^ bit] + moved.astype(F32)
        bit //= 2

    return pl.pallas_call(
        functools.partial(finish_kernel, factor),
        out_shape=jax.ShapeDtypeStruct((occ_loc, walkers, width), F32),
        in_specs=[VMEM] * (4 + len(came)),
        compiler_params=pltpu.CompilerParams(vmem_limit_bytes=4 << 20),
        name="finish",
    )(near_keep, near_got, near_came, crossed[0], *came)


def local(chol_rot, green):
    occ_loc, width = chol_rot.shape[1], green.shape[2]
    n_chol = lax.axis_size("chol")
    fits = (
        lax.axis_size("occ") == 4
        and n_chol > 1
        and n_chol & (n_chol - 1) == 0
        and width % 128 == 0
        and occ_loc % 16 == 0
        and green.shape[0] * occ_loc % 32 == 0
        and (chol_rot.shape[0] * occ_loc) % 128 == 0
    )
    return relative(chol_rot, green) if fits else general(chol_rot, green)


def solution(mesh):
    return jax.shard_map(
        local,
        mesh=mesh,
        in_specs=(P(("groups", "chol"), "occ", None), P("groups", "occ", "chol")),
        out_specs=P("occ", "groups", "chol"),
        check_vma=False,
    )
```

```python
import functools
import math

import jax
import jax.numpy as jnp
from jax import lax
from jax.experimental import pallas as pl
from jax.experimental.pallas import tpu as pltpu
from jax.sharding import PartitionSpec as P


BF16 = jnp.bfloat16
F32 = jnp.float32


def general(chol_rot, green):
    chol_loc, occ_loc, orbitals = chol_rot.shape
    walkers = green.shape[0]
    occupied = occ_loc * lax.axis_size("occ")
    nvec = chol_loc * lax.axis_size("chol")
    factor = -math.sqrt(orbitals / (nvec * occupied))
    vec_mat = chol_rot.reshape(chol_loc * occ_loc, orbitals)
    green_all = lax.all_gather(green, "occ", axis=1, tiled=True)
    piece = lax.all_gather(green_all, "chol", axis=2, tiled=True)
    flat = piece.reshape(-1, piece.shape[2])
    pair_sum = jnp.dot(vec_mat, flat.T, preferred_element_type=F32)
    pairs = pair_sum.astype(BF16).reshape(chol_loc, occ_loc, walkers, occupied)
    swapped = lax.all_to_all(pairs, "occ", split_axis=3, concat_axis=1, tiled=True)
    partial = jnp.einsum("gjwi,gip->jwp", swapped, chol_rot, preferred_element_type=F32)
    occ_summed = lax.psum_scatter(
        partial.astype(BF16), "occ", scatter_dimension=0, tiled=True
    ).astype(F32)
    summed = lax.psum_scatter(occ_summed, "chol", scatter_dimension=2, tiled=True)
    return summed * factor


def xor_permute(x, axis, bits):
    size = lax.axis_size(axis)
    return lax.ppermute(x, axis, [(i, i ^ bits) for i in range(size)])


def after(x, earlier):
    return lax.optimization_barrier((x, earlier))[0]


VMEM = pl.BlockSpec(memory_space=pltpu.VMEM)
SMEM = pl.BlockSpec(memory_space=pltpu.SMEM)


def stage_kernel(from_ref, to_ref, sem):
    copy = pltpu.make_async_copy(from_ref, to_ref, sem)
    copy.start()
    copy.wait()


def stage(x):
    return pl.pallas_call(
        stage_kernel,
        out_shape=jax.ShapeDtypeStruct(x.shape, x.dtype),
        in_specs=[pl.BlockSpec(memory_space=pltpu.HBM)],
        out_specs=VMEM,
        scratch_shapes=[pltpu.SemaphoreType.DMA],
        compiler_params=pltpu.CompilerParams(vmem_limit_bytes=4 << 20),
        cost_estimate=pl.CostEstimate(flops=0, bytes_accessed=4 * x.size, transcendentals=0),
        name="stage",
    )(x)


def store_pairs(out_ref, core, sums, walkers, occ_loc):
    for w in range(walkers):
        tiles = [
            sums[start : start + occ_loc, w * occ_loc : (w + 1) * occ_loc]
            for start in range(0, sums.shape[0], occ_loc)
        ]
        first = (core * walkers + w) * occ_loc
        out_ref[first : first + occ_loc, :] = jnp.concatenate(tiles, axis=1)


CONTRACT_LAST = (((1,), (1,)), ((), ()))


def pair_kernel(walkers, occ_loc, blocks, where_ref, own_ref, sib_ref, *refs):
    green_refs, (near_ref, sums_ref, flat) = refs[: 2 * blocks - 1], refs[2 * blocks - 1 :]
    width = flat.shape[1] // blocks
    rows = walkers * occ_loc
    total = own_ref.shape[0]
    for n in range(2 * blocks):
        side, r = divmod(n, blocks)
        start = pl.multiple_of((where_ref[0] ^ r) * width, width)
        piece = green_refs[n][...] if n < 2 * blocks - 1 else jnp.zeros((rows, width), BF16)
        flat[pl.ds(side * rows, rows), pl.ds(start, width)] = piece
    for core, vec_ref in enumerate((own_ref, sib_ref)):
        sums = lax.dot_general(vec_ref[...], flat[...], CONTRACT_LAST, preferred_element_type=F32)
        store_pairs(near_ref, core, sums[:, :rows].astype(BF16), walkers, occ_loc)
        sums_ref[core * total : (core + 1) * total, :] = sums[:, rows:]


def last_pair_kernel(walkers, occ_loc, last, where_ref, own_ref, sib_ref, green_ref, sums_ref, far_ref):
    width = green_ref.shape[1]
    total = own_ref.shape[0]
    start = pl.multiple_of((where_ref[0] ^ last) * width, width)
    for core, vec_ref in enumerate((own_ref, sib_ref)):
        sums = sums_ref[core * total : (core + 1) * total, :] + lax.dot_general(
            vec_ref[:, pl.ds(start, width)], green_ref[...], CONTRACT_LAST, preferred_element_type=F32
        )
        store_pairs(far_ref, core, sums.astype(BF16), walkers, occ_loc)


def pair_products(where, own, sib, near, far, walkers, occ_loc):
    total, orbitals = own.shape
    rows = walkers * occ_loc
    blocks = len(near)
    greens = [side[r] for side in (near, far) for r in range(blocks)]
    pairs = jax.ShapeDtypeStruct((2 * rows, total), BF16)
    sums = jax.ShapeDtypeStruct((2 * total, rows), F32)
    flops = 8 * total * orbitals * rows
    first = pl.pallas_call(
        functools.partial(pair_kernel, walkers, occ_loc, blocks),
        out_shape=(pairs, sums),
        in_specs=[SMEM] + [VMEM] * (1 + 2 * blocks),
        out_specs=(VMEM, VMEM),
        scratch_shapes=[pltpu.VMEM((2 * rows, orbitals), BF16)],
        compiler_params=pltpu.CompilerParams(vmem_limit_bytes=14 << 20),
        cost_estimate=pl.CostEstimate(
            flops=flops, bytes_accessed=4 * total * orbitals + 4 * rows * orbitals + 4 * sums.size, transcendentals=0
        ),
        name="pairs",
    )
    second = pl.pallas_call(
        functools.partial(last_pair_kernel, walkers, occ_loc, blocks - 1),
        out_shape=pairs,
        in_specs=[SMEM] + [VMEM] * 4,
        out_specs=VMEM,
        compiler_params=pltpu.CompilerParams(vmem_limit_bytes=10 << 20),
        cost_estimate=pl.CostEstimate(
            flops=flops // (2 * blocks), bytes_accessed=4 * total * orbitals // blocks + 4 * sums.size, transcendentals=0
        ),
        name="last_pairs",
    )
    stay, begun = first(where, own, sib, *greens[:-1])
    leave = second(where, own, sib, greens[-1], begun)
    return stay, leave


def partial_kernel(which, where_ref, left_ref, vec_ref, keep_ref, send_ref):
    width = keep_ref.shape[1]
    rows = left_ref.shape[0] // 2
    for n, r in enumerate(which):
        start = pl.multiple_of((where_ref[0] ^ r) * width, width)
        sums = jnp.dot(left_ref[...], vec_ref[:, pl.ds(start, width)], preferred_element_type=F32).astype(BF16)
        keep_ref[n * rows : (n + 1) * rows, :] = sums[:rows]
        send_ref[n * rows : (n + 1) * rows, :] = sums[rows:]


def partial_products(which, where, left, own, width):
    rows, total = left.shape
    out = jax.ShapeDtypeStruct((rows // 2 * len(which), width), BF16)
    call = pl.pallas_call(
        functools.partial(partial_kernel, which),
        out_shape=(out, out),
        in_specs=[SMEM, VMEM, VMEM],
        out_specs=(VMEM, VMEM),
        compiler_params=pltpu.CompilerParams(vmem_limit_bytes=10 << 20),
        cost_estimate=pl.CostEstimate(
            flops=4 * out.size * total,
            bytes_accessed=2 * rows * total + 2 * total * width * len(which) + 4 * out.size,
            transcendentals=0,
        ),
        name="partial",
    )
    keep, send = call(where, left, own)
    return keep, xor_permute(send, "occ", 1)


def finish_kernel(factor, keep_ref, got_ref, *refs):
    out_ref = refs[-1]
    occ_loc, walkers, _ = out_ref.shape
    rows = walkers * occ_loc
    total = keep_ref[-rows:].astype(F32) + got_ref[-rows:].astype(F32)
    for ref in refs[:-1]:
        total = total + ref[-rows:].astype(F32)
    total = total * factor
    for w in range(walkers):
        out_ref[:, w, :] = total[w * occ_loc : (w + 1) * occ_loc]


def relative(chol_rot, green):
    chol_loc, occ_loc, orbitals = chol_rot.shape
    walkers, _, width = green.shape
    n_chol = lax.axis_size("chol")
    occupied = occ_loc * lax.axis_size("occ")
    factor = -math.sqrt(orbitals / (chol_loc * n_chol * occupied))
    total = chol_loc * occ_loc
    rows = walkers * occ_loc

    where = lax.axis_index("chol").astype(jnp.int32).reshape(1)
    chol_rot, green = after(chol_rot, where), after(green, where)
    sib = xor_permute(chol_rot.reshape(total, orbitals), "occ", 1)
    near = {0: green.reshape(rows, width)}
    far = {0: xor_permute(near[0], "occ", 2)}
    own = stage(after(chol_rot.reshape(total, orbitals), far[0]))
    bit = n_chol // 2
    while bit:
        near |= {r | bit: xor_permute(piece, "chol", bit) for r, piece in near.items()}
        bit //= 2
    for r in range(1, n_chol):
        if r & 1:
            far[r] = xor_permute(far[r - 1], "chol", 1)
        else:
            far[r] = xor_permute(near[r], "occ", 2)
    stay, leave = pair_products(where, own, sib, near, far, walkers, occ_loc)
    come = xor_permute(leave, "occ", 2)

    odds = tuple(range(n_chol - 1, 0, -2))
    evens = tuple(r - 1 for r in odds)

    def part(x, n):
        return x[n * rows : (n + 1) * rows].astype(F32)

    odd_keep, odd_got = partial_products(odds, where, stay, own, width)
    near_keep, near_got = partial_products(evens, where, stay, own, width)
    near_odd = (odd_keep.astype(F32) + odd_got.astype(F32)).astype(BF16)
    come = after(come, (near_odd, near_keep))
    near_came = xor_permute(near_odd, "chol", 1)
    far = {}
    for which in (odds[:1], odds[1:] + evens):
        pair = partial_products(which, where, come, own, width)
        far |= {r: part(pair[0], n) + part(pair[1], n) for n, r in enumerate(which)}
    far |= {r - 1: far[r - 1] + xor_permute(far[r].astype(BF16), "chol", 1).astype(F32) for r in odds}
    crossed = {r: xor_permute(far[r].astype(BF16), "occ", 2) for r in evens}
    summed = {
        r: part(near_keep, n) + part(near_got, n) + part(near_came, n)
        + crossed[r].astype(F32)
        for n, r in enumerate(evens) if r
    }
    came = []
    bit = n_chol // 2
    while bit > 1:
        for r in evens:
            if r & bit and r < 2 * bit:
                moved = xor_permute(summed[r].astype(BF16), "chol", bit)
                if r == bit:
                    came.append(moved)
                else:
                    summed[r ^ bit] = summed[r ^ bit] + moved.astype(F32)
        bit //= 2

    return pl.pallas_call(
        functools.partial(finish_kernel, factor),
        out_shape=jax.ShapeDtypeStruct((occ_loc, walkers, width), F32),
        in_specs=[VMEM] * (4 + len(came)),
        compiler_params=pltpu.CompilerParams(vmem_limit_bytes=4 << 20),
        name="finish",
    )(near_keep, near_got, near_came, crossed[0], *came)


def local(chol_rot, green):
    occ_loc, width = chol_rot.shape[1], green.shape[2]
    n_chol = lax.axis_size("chol")
    fits = (
        lax.axis_size("occ") == 4
        and n_chol > 1
        and n_chol & (n_chol - 1) == 0
        and width % 128 == 0
        and occ_loc % 16 == 0
        and green.shape[0] * occ_loc % 32 == 0
        and (chol_rot.shape[0] * occ_loc) % 128 == 0
    )
    return relative(chol_rot, green) if fits else general(chol_rot, green)


def solution(mesh):
    return jax.shard_map(
        local,
        mesh=mesh,
        in_specs=(P(("groups", "chol"), "occ", None), P("groups", "occ", "chol")),
        out_specs=P("occ", "groups", "chol"),
        check_vma=False,
    )
```

```python
import functools
import math

import jax
import jax.numpy as jnp
from jax import lax
from jax.experimental import pallas as pl
from jax.experimental.pallas import tpu as pltpu
from jax.sharding import PartitionSpec as P


BF16 = jnp.bfloat16
F32 = jnp.float32


def general(chol_rot, green):
    chol_loc, occ_loc, orbitals = chol_rot.shape
    walkers = green.shape[0]
    occupied = occ_loc * lax.axis_size("occ")
    nvec = chol_loc * lax.axis_size("chol")
    factor = -math.sqrt(orbitals / (nvec * occupied))
    vec_mat = chol_rot.reshape(chol_loc * occ_loc, orbitals)
    green_all = lax.all_gather(green, "occ", axis=1, tiled=True)
    piece = lax.all_gather(green_all, "chol", axis=2, tiled=True)
    flat = piece.reshape(-1, piece.shape[2])
    pair_sum = jnp.dot(vec_mat, flat.T, preferred_element_type=F32)
    pairs = pair_sum.astype(BF16).reshape(chol_loc, occ_loc, walkers, occupied)
    swapped = lax.all_to_all(pairs, "occ", split_axis=3, concat_axis=1, tiled=True)
    partial = jnp.einsum("gjwi,gip->jwp", swapped, chol_rot, preferred_element_type=F32)
    occ_summed = lax.psum_scatter(
        partial.astype(BF16), "occ", scatter_dimension=0, tiled=True
    ).astype(F32)
    summed = lax.psum_scatter(occ_summed, "chol", scatter_dimension=2, tiled=True)
    return summed * factor


def xor_permute(x, axis, bits):
    size = lax.axis_size(axis)
    return lax.ppermute(x, axis, [(i, i ^ bits) for i in range(size)])


def after(x, earlier):
    return lax.optimization_barrier((x, earlier))[0]


VMEM = pl.BlockSpec(memory_space=pltpu.VMEM)
SMEM = pl.BlockSpec(memory_space=pltpu.SMEM)


def stage_kernel(from_ref, to_ref, sem):
    copy = pltpu.make_async_copy(from_ref, to_ref, sem)
    copy.start()
    copy.wait()


def stage(x):
    return pl.pallas_call(
        stage_kernel,
        out_shape=jax.ShapeDtypeStruct(x.shape, x.dtype),
        in_specs=[pl.BlockSpec(memory_space=pltpu.HBM)],
        out_specs=VMEM,
        scratch_shapes=[pltpu.SemaphoreType.DMA],
        compiler_params=pltpu.CompilerParams(vmem_limit_bytes=4 << 20),
        cost_estimate=pl.CostEstimate(flops=0, bytes_accessed=4 * x.size, transcendentals=0),
        name="stage",
    )(x)


def store_pairs(out_refs, core, sums, walkers, occ_loc):
    share = walkers // len(out_refs)
    for w in range(walkers):
        tiles = [
            sums[start : start + occ_loc, w * occ_loc : (w + 1) * occ_loc]
            for start in range(0, sums.shape[0], occ_loc)
        ]
        first = (core * share + w % share) * occ_loc
        out_refs[w // share][first : first + occ_loc, :] = jnp.concatenate(tiles, axis=1)


CONTRACT_LAST = (((1,), (1,)), ((), ()))


def pair_kernel(walkers, occ_loc, blocks, where_ref, own_ref, sib_ref, *refs):
    green_refs, (near_ref, sums_ref, flat) = refs[: 2 * blocks - 1], refs[2 * blocks - 1 :]
    width = flat.shape[1] // blocks
    rows = walkers * occ_loc
    total = own_ref.shape[0]
    for n in range(2 * blocks):
        side, r = divmod(n, blocks)
        start = pl.multiple_of((where_ref[0] ^ r) * width, width)
        piece = green_refs[n][...] if n < 2 * blocks - 1 else jnp.zeros((rows, width), BF16)
        flat[pl.ds(side * rows, rows), pl.ds(start, width)] = piece
    for core, vec_ref in enumerate((own_ref, sib_ref)):
        sums = lax.dot_general(vec_ref[...], flat[...], CONTRACT_LAST, preferred_element_type=F32)
        store_pairs((near_ref,), core, sums[:, :rows].astype(BF16), walkers, occ_loc)
        sums_ref[core * total : (core + 1) * total, :] = sums[:, rows:]


def last_pair_kernel(walkers, occ_loc, last, where_ref, own_ref, sib_ref, green_ref, sums_ref, *far_refs):
    width = green_ref.shape[1]
    total = own_ref.shape[0]
    start = pl.multiple_of((where_ref[0] ^ last) * width, width)
    for core, vec_ref in enumerate((own_ref, sib_ref)):
        sums = sums_ref[core * total : (core + 1) * total, :] + lax.dot_general(
            vec_ref[:, pl.ds(start, width)], green_ref[...], CONTRACT_LAST, preferred_element_type=F32
        )
        store_pairs(far_refs, core, sums.astype(BF16), walkers, occ_loc)


def pair_products(where, own, sib, near, far, walkers, occ_loc):
    total, orbitals = own.shape
    rows = walkers * occ_loc
    blocks = len(near)
    greens = [side[r] for side in (near, far) for r in range(blocks)]
    pairs = jax.ShapeDtypeStruct((2 * rows, total), BF16)
    half = jax.ShapeDtypeStruct((rows, total), BF16)
    sums = jax.ShapeDtypeStruct((2 * total, rows), F32)
    flops = 8 * total * orbitals * rows
    first = pl.pallas_call(
        functools.partial(pair_kernel, walkers, occ_loc, blocks),
        out_shape=(pairs, sums),
        in_specs=[SMEM] + [VMEM] * (1 + 2 * blocks),
        out_specs=(VMEM, VMEM),
        scratch_shapes=[pltpu.VMEM((2 * rows, orbitals), BF16)],
        compiler_params=pltpu.CompilerParams(vmem_limit_bytes=14 << 20),
        cost_estimate=pl.CostEstimate(
            flops=flops, bytes_accessed=4 * total * orbitals + 4 * rows * orbitals + 4 * sums.size, transcendentals=0
        ),
        name="pairs",
    )
    second = pl.pallas_call(
        functools.partial(last_pair_kernel, walkers, occ_loc, blocks - 1),
        out_shape=(half, half),
        in_specs=[SMEM] + [VMEM] * 4,
        out_specs=(VMEM, VMEM),
        compiler_params=pltpu.CompilerParams(vmem_limit_bytes=10 << 20),
        cost_estimate=pl.CostEstimate(
            flops=flops // (2 * blocks), bytes_accessed=4 * total * orbitals // blocks + 4 * sums.size, transcendentals=0
        ),
        name="last_pairs",
    )
    stay, begun = first(where, own, sib, *greens[:-1])
    leave = second(where, own, sib, greens[-1], begun)
    return stay, leave


def partial_kernel(which, where_ref, left_ref, vec_ref, keep_ref, send_ref):
    width = keep_ref.shape[1]
    rows = left_ref.shape[0] // 2
    for n, r in enumerate(which):
        start = pl.multiple_of((where_ref[0] ^ r) * width, width)
        sums = jnp.dot(left_ref[...], vec_ref[:, pl.ds(start, width)], preferred_element_type=F32).astype(BF16)
        keep_ref[n * rows : (n + 1) * rows, :] = sums[:rows]
        send_ref[n * rows : (n + 1) * rows, :] = sums[rows:]


def partial_products(which, where, left, own, width):
    rows, total = left.shape
    out = jax.ShapeDtypeStruct((rows // 2 * len(which), width), BF16)
    call = pl.pallas_call(
        functools.partial(partial_kernel, which),
        out_shape=(out, out),
        in_specs=[SMEM, VMEM, VMEM],
        out_specs=(VMEM, VMEM),
        compiler_params=pltpu.CompilerParams(vmem_limit_bytes=10 << 20),
        cost_estimate=pl.CostEstimate(
            flops=4 * out.size * total,
            bytes_accessed=2 * rows * total + 2 * total * width * len(which) + 4 * out.size,
            transcendentals=0,
        ),
        name="partial",
    )
    keep, send = call(where, left, own)
    return keep, xor_permute(send, "occ", 1)


def near_sum_kernel(*refs):
    rows, _ = refs[-1].shape
    total = refs[0][-rows:].astype(F32)
    for ref in refs[1:-1]:
        total = total + ref[-rows:].astype(F32)
    refs[-1][...] = total


def near_sum(near, rows):
    width = near[0].shape[1]
    return pl.pallas_call(
        near_sum_kernel,
        out_shape=jax.ShapeDtypeStruct((rows, width), F32),
        in_specs=[VMEM] * len(near),
        out_specs=VMEM,
        compiler_params=pltpu.CompilerParams(vmem_limit_bytes=4 << 20),
        cost_estimate=pl.CostEstimate(flops=3 * rows * width, bytes_accessed=10 * rows * width, transcendentals=0),
        name="near_sum",
    )(*near)


def finish_kernel(factor, halves, base_ref, crossed_ref, *refs):
    out_ref = refs[-1]
    occ_loc, walkers, _ = out_ref.shape
    total = base_ref[...] + crossed_ref[...].astype(F32)
    chunk = total.shape[0] // 2
    sums = [total[:chunk], total[chunk:]]
    for h, ref in zip(halves, refs[:-1]):
        sums[h] = sums[h] + ref[...].astype(F32)
    share = walkers // 2
    for w in range(walkers):
        first = w % share * occ_loc
        out_ref[:, w, :] = sums[w // share][first : first + occ_loc] * factor


def relative(chol_rot, green):
    chol_loc, occ_loc, orbitals = chol_rot.shape
    walkers, _, width = green.shape
    n_chol = lax.axis_size("chol")
    occupied = occ_loc * lax.axis_size("occ")
    factor = -math.sqrt(orbitals / (chol_loc * n_chol * occupied))
    total = chol_loc * occ_loc
    rows = walkers * occ_loc

    where = lax.axis_index("chol").astype(jnp.int32).reshape(1)
    chol_rot, green = after(chol_rot, where), after(green, where)
    sib = xor_permute(chol_rot.reshape(total, orbitals), "occ", 1)
    near = {0: green.reshape(rows, width)}
    far = {0: xor_permute(near[0], "occ", 2)}
    own = stage(after(chol_rot.reshape(total, orbitals), far[0]))
    bit = n_chol // 2
    while bit:
        near |= {r | bit: xor_permute(piece, "chol", bit) for r, piece in near.items()}
        bit //= 2
    for r in range(1, n_chol):
        if r & 1:
            far[r] = xor_permute(far[r - 1], "chol", 1)
        else:
            far[r] = xor_permute(near[r], "occ", 2)
    stay, leave = pair_products(where, own, sib, near, far, walkers, occ_loc)
    come = [xor_permute(x, "occ", 2) for x in leave]

    odds = tuple(range(n_chol - 1, 0, -2))
    evens = tuple(r - 1 for r in odds)
    chunk = rows // 2

    def part(x, n):
        return x[n * chunk : (n + 1) * chunk].astype(F32)

    odd_keep, odd_got = partial_products(odds, where, stay, own, width)
    near_keep, near_got = partial_products(evens, where, stay, own, width)
    near_odd = (odd_keep.astype(F32) + odd_got.astype(F32)).astype(BF16)
    near_came = xor_permute(near_odd, "chol", 1)
    near = (near_keep, near_got, near_came)
    earlier = (near_odd, near_keep)
    far, pairs = [], []
    for h in range(2):
        pair = partial_products(odds + evens, where, after(come[h], earlier), own, width)
        earlier = pair[0]
        pairs.append(pair)
        far.append({r: part(pair[0], n) + part(pair[1], n) for n, r in enumerate(odds + evens)})

    crossed, sent = [{}, {}], near_odd
    for h in range(2):
        for r in evens:
            if r:
                moved = xor_permute(far[h][r + 1].astype(BF16), "chol", 1)
                moved = after(moved, sent)
                sent = (far[h][r] + moved.astype(F32)).astype(BF16)
                crossed[h][r] = xor_permute(sent, "occ", 2)
    n_one, n_zero = (odds + evens).index(1), (odds + evens).index(0)
    gated = [tuple(after(x, sent) for x in pair) for pair in pairs]

    def both(n):
        return jnp.concatenate([part(keep, n) + part(got, n) for keep, got in gated])

    moved = xor_permute(both(n_one).astype(BF16), "chol", 1)
    first_crossed = xor_permute((both(n_zero) + moved.astype(F32)).astype(BF16), "occ", 2)
    came = []
    for h in range(2):
        summed = {}
        for n, r in enumerate(evens):
            if r:
                summed[r] = after(crossed[h][r], sent).astype(F32)
                for x in near:
                    summed[r] = summed[r] + part(x, 2 * n + h)
        bit = n_chol // 2
        while bit > 1:
            for r in evens:
                if r & bit and r < 2 * bit:
                    sent = summed[r].astype(BF16)
                    moved = xor_permute(sent, "chol", bit)
                    if r == bit:
                        came.append((h, moved))
                    else:
                        summed[r ^ bit] = summed[r ^ bit] + moved.astype(F32)
            bit //= 2

    return pl.pallas_call(
        functools.partial(finish_kernel, factor, tuple(h for h, _ in came)),
        out_shape=jax.ShapeDtypeStruct((occ_loc, walkers, width), F32),
        in_specs=[VMEM] * (2 + len(came)),
        compiler_params=pltpu.CompilerParams(vmem_limit_bytes=4 << 20),
        name="finish",
    )(near_sum(near, rows), first_crossed, *(x for _, x in came))


def local(chol_rot, green):
    occ_loc, width = chol_rot.shape[1], green.shape[2]
    n_chol = lax.axis_size("chol")
    fits = (
        lax.axis_size("occ") == 4
        and n_chol > 1
        and n_chol & (n_chol - 1) == 0
        and width % 128 == 0
        and occ_loc % 16 == 0
        and green.shape[0] % 2 == 0
        and (chol_rot.shape[0] * occ_loc) % 128 == 0
    )
    return relative(chol_rot, green) if fits else general(chol_rot, green)


def solution(mesh):
    return jax.shard_map(
        local,
        mesh=mesh,
        in_specs=(P(("groups", "chol"), "occ", None), P("groups", "occ", "chol")),
        out_specs=P("occ", "groups", "chol"),
        check_vma=False,
    )
```
